32 devices in a mesh: seq: 16 (over z, x, core), head: 2 (over y).
Axes of the slice: x: 2, y: 2, z: 4, core: 2. Of those that a mesh axis runs over, the one named last changes fastest.
Arguments:
- queries: bfloat16 [12288, 4096], P('seq', 'head'), may hold values from -100 to 100
- keys: bfloat16 [12288, 4096], P('seq', 'head'), may hold values from -7 to 7
- values: bfloat16 [12288, 4096], P('seq', 'head'), may hold values from -6 to 6
- targets: bfloat16 [12288, 4096], P('seq', 'head'), may hold values from -6 to 6
- token_rate: float32 [12288, 8], P('seq', 'head'), may hold values from 0.1 to 1
- window: int32 [8], P('head'), may hold values from 256 to 512, as said below
- split: int32 [1], replicated, may hold values from 4608 to 7679
- fast_init: float32 [8, 3, 512, 512], P('head'), may hold values from -0.25 to 0.25
Outputs:
- mixed: bfloat16 [12288, 4096], P('seq', 'head')
- fast_final: float32 [8, 3, 512, 512], P('head')
The draws below stay inside these ranges and needn't reach their ends.
Inputs may be any that keep to these rules, and one draw needn't show every extreme that they name: Some head has a window of exactly 512.
All inputs are finite; a program needn't handle non-finite values.
Results may differ from the reference program's by a relative error of at most 0.0073.
Values may be sent and summed in bfloat16 or wider, within the bound.
A program may use at most 192 MiB of HBM per device.

```python
import math
import jax
import jax.numpy as jnp
from jax import lax

HEADS = 8
HD = 512
HID = 512
WIN = 512
TOKENS = 12288


def joint_draw(key):
    base = jax.random.fold_in(key, 11)
    key_a, key_b = jax.random.split(base, 2)
    shape = (TOKENS, HEADS * HD)
    keys = jax.random.truncated_normal(key_a, -6.0, 6.0, shape, jnp.float32)
    queries = jax.random.truncated_normal(key_b, -6.0, 6.0, shape, jnp.float32)
    return (queries, keys)


def draw_queries(key, part):
    return joint_draw(key)[0].astype(jnp.bfloat16)


def draw_keys(key, part):
    return joint_draw(key)[1].astype(jnp.bfloat16)


def draw_window(key, part):
    base = jax.random.fold_in(key, 23)
    key_a, key_b = jax.random.split(base)
    widths = jax.random.randint(key_a, (HEADS,), WIN // 2, WIN + 1)
    chosen = jax.random.randint(key_b, (), 0, HEADS)
    return jnp.where(jnp.arange(HEADS) == chosen, WIN, widths).astype(jnp.int32)


def block_levels(stream_key, extent, cuts, low, high):
    loudness = 1.0
    for axis_at, parts in cuts:
        draws = jax.random.uniform(jax.random.fold_in(jax.random.fold_in(stream_key, 6), axis_at), (parts,), jnp.float32, low / len(cuts), high / len(cuts))
        loudness = loudness * jnp.repeat(jnp.exp(draws), extent[axis_at] // parts).reshape((-1,) + (1,) * (len(extent) - 1 - axis_at))
    return loudness


def bell_draw(key, shape, spread, most, pieces=(), kind=jnp.bfloat16):
    values = spread * jax.random.normal(key, shape, jnp.float32)
    if pieces:
        values = values * block_levels(key, shape, pieces, -0.22, 0.18)
    return jnp.clip(values, -most, most).astype(kind)


def setup_inputs(seed: int = 0) -> dict:
    seeds = jax.random.split(jax.random.key(seed), 9)
    return {
        "queries": draw_queries(jax.random.fold_in(seeds[8], 71), 0),
        "keys": draw_keys(jax.random.fold_in(seeds[8], 71), 0),
        "values": bell_draw(seeds[2], (TOKENS, HEADS * HD), 1.0, 6.0, ((0, 16), (1, 2))),
        "targets": bell_draw(seeds[3], (TOKENS, HEADS * HD), 1.0, 6.0, ((0, 16), (1, 2))),
        "token_rate": jnp.clip(jnp.exp(math.log(1.0) - 2.3025851 * jax.random.uniform(seeds[4], (TOKENS, HEADS), jnp.float32) ** block_levels(seeds[4], (TOKENS, HEADS), ((0, 16), (1, 2)), -0.2, 0.2)), 0.1, 1.0),
        "window": draw_window(jax.random.fold_in(seeds[8], 71), 0),
        "split": jax.random.randint(seeds[6], (1,), TOKENS // 2 - TOKENS // 8, TOKENS // 2 + TOKENS // 8).astype(jnp.int32),
        "fast_init": bell_draw(seeds[7], (HEADS, 3, HD, HID), HD ** -0.5, 0.25, ((0, 2),), jnp.float32),
    }


fast_rate = 0.01
epsilon = 1e-06

def fast_apply(inputs, weights):
    first = jnp.dot(inputs, weights[0], preferred_element_type=jnp.float32)
    third = jnp.dot(inputs, weights[1], preferred_element_type=jnp.float32)
    act = (jax.nn.silu(first) * third).astype(jnp.bfloat16)
    return lax.dot_general(act, weights[2], (((1,), (1,)), ((), ())), preferred_element_type=jnp.float32)

def fast_grad(inputs, targets, scaled, weights):
    first = jnp.dot(inputs, weights[0], preferred_element_type=jnp.float32)
    third = jnp.dot(inputs, weights[1], preferred_element_type=jnp.float32)
    sigma = jax.nn.sigmoid(first)
    swish = first * sigma
    act = (swish * third).astype(jnp.bfloat16)
    d_out = (-scaled * targets.astype(jnp.float32)).astype(jnp.bfloat16)
    d_act = jnp.dot(d_out, weights[2], preferred_element_type=jnp.float32)
    d_first = (d_act * third * sigma * (1.0 + first * (1.0 - sigma))).astype(jnp.bfloat16)
    d_third = (d_act * swish).astype(jnp.bfloat16)
    dims = (((0,), (0,)), ((), ()))
    grad_one = lax.dot_general(inputs, d_first, dims, preferred_element_type=jnp.float32)
    grad_three = lax.dot_general(inputs, d_third, dims, preferred_element_type=jnp.float32)
    grad_two = lax.dot_general(d_out, act, dims, preferred_element_type=jnp.float32)
    return jnp.stack([grad_one, grad_three, grad_two])

def attend_head(query_head, key_head, value_head, width):
    total = query_head.shape[0]
    block = math.gcd(total, 512)
    pad = jnp.zeros((WIN, HD), jnp.bfloat16)
    key_pad = jnp.concatenate([pad, key_head], axis=0)
    value_pad = jnp.concatenate([pad, value_head], axis=0)
    scale = HD ** (-0.5)

    def one_block(start):
        query_block = lax.dynamic_slice_in_dim(query_head, start, block, 0)
        key_block = lax.dynamic_slice_in_dim(key_pad, start, block + WIN, 0)
        value_block = lax.dynamic_slice_in_dim(value_pad, start, block + WIN, 0)
        scores = lax.dot_general(query_block, key_block, (((1,), (1,)), ((), ())), preferred_element_type=jnp.float32) * scale
        query_pos = start + jnp.arange(block, dtype=jnp.int32)[:, None]
        key_pos = start - WIN + jnp.arange(block + WIN, dtype=jnp.int32)[None, :]
        live = (key_pos <= query_pos) & (key_pos > query_pos - width) & (key_pos >= 0)
        scores = jnp.where(live, scores, -1e+30)
        peak = lax.optimization_barrier(jnp.max(scores, axis=1, keepdims=True))
        expo = jnp.where(live, jnp.exp(scores - peak), 0.0)
        probs = (expo / lax.optimization_barrier(jnp.sum(expo, axis=1, keepdims=True))).astype(jnp.bfloat16)
        return jnp.dot(probs, value_block, preferred_element_type=jnp.float32)
    starts = jnp.arange(total // block, dtype=jnp.int32) * block
    return lax.map(one_block, starts).reshape(total, HD)

def renew_weights(weights, grads):
    square = jnp.sum(grads * grads)
    count = float(HEADS * 3 * HD * HID)
    return weights - fast_rate / jnp.sqrt(square / count + epsilon) * grads

def reference(queries, keys, values, targets, token_rate, window, split, fast_init):
    positions = jnp.arange(TOKENS, dtype=jnp.int32)[:, None]
    first_block = (positions < split[0]).astype(jnp.float32)
    second_block = 1.0 - first_block

    def column(array, head):
        return lax.dynamic_slice_in_dim(array, head * HD, HD, 1)

    def grads_of(weights, mask):

        def per_head(head):
            scaled = lax.dynamic_slice_in_dim(token_rate, head, 1, 1) * mask
            return fast_grad(column(keys, head), column(targets, head), scaled, weights[head].astype(jnp.bfloat16))
        return lax.map(per_head, jnp.arange(HEADS, dtype=jnp.int32))
    weights_zero = fast_init
    weights_one = renew_weights(weights_zero, grads_of(weights_zero, first_block))
    weights_two = renew_weights(weights_one, grads_of(weights_one, second_block))

    def output_head(head):
        query_head = column(queries, head)
        attn = attend_head(query_head, column(keys, head), column(values, head), window[head])
        early = fast_apply(query_head, weights_zero[head].astype(jnp.bfloat16))
        late = fast_apply(query_head, weights_one[head].astype(jnp.bfloat16))
        fast_out = first_block * early + second_block * late
        normed = fast_out / jnp.sqrt(lax.optimization_barrier(jnp.mean(fast_out * fast_out, axis=1, keepdims=True)) + epsilon)
        return (attn + normed).astype(jnp.bfloat16)
    heads_out = lax.map(output_head, jnp.arange(HEADS, dtype=jnp.int32))
    mixed = jnp.transpose(heads_out, (1, 0, 2)).reshape(TOKENS, HEADS * HD)
    return (mixed, weights_two)
```

```python
import functools

import jax
import jax.numpy as jnp
from jax import lax
from jax.experimental import pallas as pl
from jax.experimental.pallas import tpu as pltpu
from jax.sharding import PartitionSpec as P

WIN = 512
fast_rate = 0.01
epsilon = 1e-06
CORES = 2


def mm(a, b, ca, cb):
    return lax.dot_general(
        a, b, (((ca,), (cb,)), ((), ())), preferred_element_type=jnp.float32
    )


def grad_kernel(renewed, info_ref, coef_ref, keys_ref, targets_ref, scaled_ref, w_ref, *rest):
    if renewed:
        g_ref, out_ref = rest
    else:
        (out_ref,) = rest
    head = pl.program_id(0)

    @pl.when(info_ref[0] == 0)
    def _():
        out_ref[...] = jnp.zeros_like(out_ref)

    @pl.when(info_ref[0] != 0)
    def _():
        def weight(i):
            w = w_ref[0, i]
            if renewed:
                w = w - coef_ref[0] * g_ref[0, i].astype(jnp.float32)
            return w.astype(jnp.bfloat16)

        x = keys_ref[...]
        column = lax.broadcasted_iota(jnp.int32, scaled_ref.shape, 1)
        scaled = jnp.sum(
            jnp.where(column == head, scaled_ref[...], 0.0), axis=1, keepdims=True
        )
        first = mm(x, weight(0), 1, 0)
        third = mm(x, weight(1), 1, 0)
        d_out = (-scaled * targets_ref[...].astype(jnp.float32)).astype(jnp.bfloat16)
        d_act = mm(d_out, weight(2), 1, 0)
        sigma = jax.nn.sigmoid(first)
        swish = first * sigma
        act = (swish * third).astype(jnp.bfloat16)
        d_first = (d_act * third * sigma * (1.0 + first * (1.0 - sigma))).astype(jnp.bfloat16)
        d_third = (d_act * swish).astype(jnp.bfloat16)
        out_ref[0, 0] = mm(x, d_first, 0, 0).astype(jnp.bfloat16)
        out_ref[0, 1] = mm(x, d_third, 0, 0).astype(jnp.bfloat16)
        out_ref[0, 2] = mm(d_out, act, 0, 0).astype(jnp.bfloat16)


def gradients(info, coef, keys, targets, scaled, weights, g):
    local = keys.shape[0]
    heads, _, hd, hid = weights.shape
    wspec = pl.BlockSpec((1, 3, hd, hid), lambda h: (h, 0, 0, 0))
    smem = pl.BlockSpec(memory_space=pltpu.SMEM)
    col = pl.BlockSpec((local, hd), lambda h: (0, h))
    args = [info, coef, keys, targets, scaled, weights]
    specs = [smem, smem, col, col, pl.BlockSpec(scaled.shape, lambda h: (0, 0)), wspec]
    if g is not None:
        args.append(g)
        specs.append(wspec)
    return pl.pallas_call(
        functools.partial(grad_kernel, g is not None),
        grid=(heads,),
        in_specs=specs,
        out_specs=wspec,
        out_shape=jax.ShapeDtypeStruct(weights.shape, jnp.bfloat16),
        compiler_params=pltpu.CompilerParams(vmem_limit_bytes=56 << 20),
        cost_estimate=pl.CostEstimate(
            flops=12 * heads * local * hd * hid, bytes_accessed=30 << 20, transcendentals=0
        ),
        name="grad",
    )(*args)


def attention_kernel(head, chained, info_ref, win_ref, q_ref, k_ref, kh_ref, v_ref, vh_ref, *rest):
    out_ref = rest[-1]
    local, hd = q_ref.shape
    block = 256
    width = win_ref[head]
    anchor = info_ref[2]
    k_all = jnp.concatenate([kh_ref[...], k_ref[...]], axis=0)
    v_all = jnp.concatenate([vh_ref[...], v_ref[...]], axis=0)
    span = WIN + block
    for start in range(0, local, block):
        scores = mm(q_ref[start : start + block], k_all[start : start + span], 1, 1) * (
            hd ** (-0.5)
        )
        row = lax.broadcasted_iota(jnp.int32, (block, span), 0)
        colm = lax.broadcasted_iota(jnp.int32, (block, span), 1)
        back = row + WIN - colm
        live = (back >= 0) & (back < width) & (colm >= WIN - start - anchor)
        scores = jnp.where(live, scores, -1e30)
        peak = jnp.max(scores, axis=1, keepdims=True)
        expo = jnp.exp(scores - peak)
        probs = (expo * (1.0 / jnp.sum(expo, axis=1, keepdims=True))).astype(jnp.bfloat16)
        out_ref[start : start + block] = mm(probs, v_all[start : start + span], 1, 0)


def attention(head, prev, info, window, q, k, kh, v, vh, heads):
    local = q.shape[0]
    hd = q.shape[1] // heads
    smem = pl.BlockSpec(memory_space=pltpu.SMEM)
    col = pl.BlockSpec((local, hd), lambda i: (0, head))
    halo = pl.BlockSpec((WIN, hd), lambda i: (0, head))
    args = [info, window, q, k, kh, v, vh]
    specs = [smem, smem, col, col, halo, col, halo]
    aliases = {}
    if prev is not None:
        args.append(prev)
        specs.append(pl.BlockSpec(memory_space=pl.ANY))
        aliases = {len(args) - 1: 0}
    return pl.pallas_call(
        functools.partial(attention_kernel, head, prev is not None),
        grid=(1,),
        in_specs=specs,
        out_specs=col,
        out_shape=jax.ShapeDtypeStruct(q.shape, jnp.float32),
        input_output_aliases=aliases,
        compiler_params=pltpu.CompilerParams(vmem_limit_bytes=40 << 20),
        cost_estimate=pl.CostEstimate(
            flops=6 * 4 * local * 768 * hd, bytes_accessed=8 << 20, transcendentals=0
        ),
        name="attend",
    )(*args)


def mix_kernel(info_ref, coef_ref, q_ref, attn_ref, w_ref, g_ref, out_ref, y_ref):
    position = info_ref[2] + lax.broadcasted_iota(jnp.int32, (q_ref.shape[0], 1), 0)
    for c in range(2):

        @pl.when(info_ref[c] != 0)
        def _():
            def weight(i):
                w = w_ref[0, i]
                if c:
                    w = w - coef_ref[0] * g_ref[0, i].astype(jnp.float32)
                return w.astype(jnp.bfloat16)

            q = q_ref[...]
            first = mm(q, weight(0), 1, 0)
            third = mm(q, weight(1), 1, 0)
            act = (first * jax.nn.sigmoid(first) * third).astype(jnp.bfloat16)
            y = mm(act, weight(2), 1, 1)
            mine = (position < info_ref[3]) == (c == 0)
            y_ref[...] = jnp.where(mine, y, y_ref[...])

    y = y_ref[...]
    mean = jnp.mean(y * y, axis=1, keepdims=True)
    out_ref[...] = (attn_ref[...] + y / jnp.sqrt(mean + epsilon)).astype(jnp.bfloat16)


def mix(info, coef, q, attn, weights, g):
    local = q.shape[0]
    heads, _, hd, hid = weights.shape
    wspec = pl.BlockSpec((1, 3, hd, hid), lambda h: (h, 0, 0, 0))
    smem = pl.BlockSpec(memory_space=pltpu.SMEM)
    col = pl.BlockSpec((local, hd), lambda h: (0, h))
    return pl.pallas_call(
        mix_kernel,
        grid=(heads,),
        in_specs=[smem, smem, col, col, wspec, wspec],
        out_specs=col,
        out_shape=jax.ShapeDtypeStruct(q.shape, jnp.bfloat16),
        scratch_shapes=[pltpu.VMEM((local, hd), jnp.float32)],
        compiler_params=pltpu.CompilerParams(vmem_limit_bytes=56 << 20),
        cost_estimate=pl.CostEstimate(
            flops=8 * heads * local * hd * hid, bytes_accessed=30 << 20, transcendentals=0
        ),
        name="mix",
    )(info, coef, q, attn, weights, g)


def add_rows(dst, parts):
    rows = dst.shape[0]
    tile = 64 if rows % 64 == 0 else 16

    @pl.loop(0, rows // tile)
    def _(i):
        at = pl.ds(pl.multiple_of(i * tile, tile), tile)
        total = parts[0][at].astype(jnp.float32)
        for part in parts[1:]:
            total += part[at].astype(jnp.float32)
        dst[at] = total.astype(dst.dtype)


def reduce_kernel(near_size, far_size, g_ref, out_ref, sq_ref, r1, s1, rn, sn, rf, sf, send, recv):
    me = lax.axis_index("seq")
    strides = (1, CORES, CORES * near_size)
    sizes = (CORES, near_size, far_size)
    places = tuple((me // st) % sz for st, sz in zip(strides, sizes))
    core, near, far = places

    def peer(axis, d):
        p = places[axis]
        return me + ((p + d) % sizes[axis] - p) * strides[axis]

    barrier = pltpu.get_barrier_semaphore()
    total = 0
    for axis in range(3):
        for d in range(1, sizes[axis]):
            pl.semaphore_signal(
                barrier,
                inc=1,
                device_id={"seq": peer(axis, d)},
                device_id_type=pl.DeviceIdType.MESH,
            )
            total += 1
    pl.semaphore_wait(barrier, total)

    used = [0]

    def copy(src, dst, axis, d):
        k = used[0]
        used[0] += 1
        c = pltpu.make_async_remote_copy(
            src_ref=src,
            dst_ref=dst,
            send_sem=send.at[k],
            recv_sem=recv.at[k],
            device_id={"seq": peer(axis, d)},
            device_id_type=pl.DeviceIdType.MESH,
        )
        c.start()
        return c

    half = g_ref.shape[0] // CORES
    width = g_ref.shape[1] // 2

    def rows(start, size):
        return pl.ds(pl.multiple_of(start, 16), size)

    other = (core + 1) % CORES
    cs = []
    for w in range(2):
        cols = pl.ds(w * width, width)
        cs.append(copy(g_ref.at[rows(other * half, half), cols], r1.at[w], 0, 1))

    def scatter(axis, src, got):
        size = sizes[axis]
        step = src.shape[0] // size
        return [
            copy(
                src.at[rows(((places[axis] + d) % size) * step, step)],
                got.at[d - 1, pl.ds(0, step)],
                axis,
                d,
            )
            for d in range(1, size)
        ]

    def settle(axis, src, got, dst, copies):
        size = sizes[axis]
        step = src.shape[0] // size
        for c in copies:
            c.wait()
        parts = [src.at[rows(places[axis] * step, step)]]
        parts += [got.at[d - 1, pl.ds(0, step)] for d in range(1, size)]
        add_rows(dst, parts)

    orders = ((1, 2), (2, 1))
    got_of = {1: rn, 2: rf}
    first = []
    for w in range(2):
        cs[w].wait()
        cols = pl.ds(w * width, width)
        add_rows(s1.at[w], [g_ref.at[rows(core * half, half), cols], r1.at[w]])
        axis = orders[w][0]
        first.append(scatter(axis, s1.at[w], got_of[axis].at[w]))
    second = []
    mids = []
    for w in range(2):
        a1, a2 = orders[w]
        mid = (sn if w == 0 else sf).at[pl.ds(0, half // sizes[a1])]
        mids.append(mid)
        settle(a1, s1.at[w], got_of[a1].at[w], mid, first[w])
        second.append(scatter(a2, mid, got_of[a2].at[w]))
    small = half // (near_size * far_size)
    third = []
    for w in range(2):
        a1, a2 = orders[w]
        cols = pl.ds(w * width, width)
        start = core * half + places[a1] * (half // sizes[a1]) + places[a2] * small
        own = out_ref.at[rows(start, small), cols]
        settle(a2, mids[w], got_of[a2].at[w], own, second[w])
        third.append([copy(own, own, a2, d) for d in range(1, sizes[a2])])
    fourth = []
    for w in range(2):
        a1, a2 = orders[w]
        cols = pl.ds(w * width, width)
        for c in third[w]:
            c.wait()
        block = half // sizes[a1]
        mine = out_ref.at[rows(core * half + places[a1] * block, block), cols]
        fourth.append([copy(mine, mine, a1, d) for d in range(1, sizes[a1])])
    last = []
    for w in range(2):
        cols = pl.ds(w * width, width)
        for c in fourth[w]:
            c.wait()
        mine = out_ref.at[rows(core * half, half), cols]
        last.append(copy(mine, mine, 0, 1))
    for c in last:
        c.wait()
    tile = 64

    def square(i, total):
        at = pl.ds(pl.multiple_of(i * tile, tile), tile)
        part = jnp.square(out_ref[at].astype(jnp.float32))
        return total + jnp.sum(part.reshape(tile // 8, 8, -1), axis=0)

    sq_ref[...] = lax.fori_loop(
        0, out_ref.shape[0] // tile, square, jnp.zeros(sq_ref.shape, jnp.float32)
    )


def summed(ident, grads, total_count):
    count = lax.axis_size("seq")
    chips = count // CORES
    near = 1
    while near * near * 4 <= chips:
        near *= 2
    far = chips // near
    flat = grads.reshape(-1, grads.shape[-1])
    half = flat.shape[0] // CORES
    width = flat.shape[1] // 2
    copies = 4 + 4 * (near - 1) + 4 * (far - 1)
    vm = lambda *shape: pltpu.VMEM(shape, jnp.bfloat16)
    vmem = pl.BlockSpec(memory_space=pltpu.VMEM)
    out, squares = pl.pallas_call(
        functools.partial(reduce_kernel, near, far),
        in_specs=[vmem],
        out_specs=(vmem, vmem),
        out_shape=(
            jax.ShapeDtypeStruct(flat.shape, flat.dtype),
            jax.ShapeDtypeStruct((8, flat.shape[1]), jnp.float32),
        ),
        scratch_shapes=[
            vm(2, half, width),
            vm(2, half, width),
            vm(2, max(near - 1, 1), half // near, width),
            vm(half // near, width),
            vm(2, max(far - 1, 1), half // far, width),
            vm(half // far, width),
            pltpu.SemaphoreType.DMA((copies,)),
            pltpu.SemaphoreType.DMA((copies,)),
        ],
        compiler_params=pltpu.CompilerParams(
            collective_id=ident, has_side_effects=True, vmem_limit_bytes=58 << 20
        ),
        cost_estimate=pl.CostEstimate(
            flops=10**11, bytes_accessed=4 * flat.size, transcendentals=0
        ),
        name="reduce",
    )(flat)
    square = lax.psum(jnp.sum(squares), "head")
    factor = fast_rate / jnp.sqrt(square / total_count + epsilon)
    return out.reshape(grads.shape), factor


def per_device(queries, keys, values, targets, token_rate, window, split, fast_init):
    local = queries.shape[0]
    heads = fast_init.shape[0]
    count = lax.axis_size("seq")
    total_count = float(fast_init.size * lax.axis_size("head"))
    anchor = (lax.axis_index("seq") * local).astype(jnp.int32)
    edge = split[0]
    early = (anchor < edge).astype(jnp.int32)
    late = (anchor + local > edge).astype(jnp.int32)
    info = jnp.stack([early, late, anchor, edge])
    info_late = jnp.stack([late, late, anchor, edge])
    positions = anchor + jnp.arange(local, dtype=jnp.int32)[:, None]
    first_block = (positions < edge).astype(jnp.float32)

    forward = [(i, i + 1) for i in range(count - 1)]
    key_halo = lax.ppermute(keys[local - WIN :], "seq", forward)
    value_halo = lax.ppermute(values[local - WIN :], "seq", forward)

    zero = jnp.zeros((1,), jnp.float32)
    g0 = gradients(info, zero, keys, targets, token_rate * first_block, fast_init, None)
    g0, c0 = summed(0, g0, total_count)
    c0, key_halo, value_halo = lax.optimization_barrier((c0, key_halo, value_halo))
    attn = None
    for head in range(heads):
        attn = attention(
            head, attn, info, window, queries, keys, key_halo, values, value_halo, heads
        )
    coef = c0.reshape(1)
    g1 = gradients(
        info_late, coef, keys, targets, token_rate * (1.0 - first_block), fast_init, g0
    )
    g1, c1 = summed(1, g1, total_count)
    mixed = mix(info, coef, queries, attn, fast_init, g0)
    weights = fast_init - c0 * g0.astype(jnp.float32) - c1 * g1.astype(jnp.float32)
    return mixed, weights


def solution(mesh):
    return jax.shard_map(
        per_device,
        mesh=mesh,
        in_specs=(
            P("seq", "head"),
            P("seq", "head"),
            P("seq", "head"),
            P("seq", "head"),
            P("seq", "head"),
            P("head"),
            P(),
            P("head", None, None, None),
        ),
        out_specs=(P("seq", "head"), P("head", None, None, None)),
        check_vma=False,
    )
```

```python
import functools

import jax
import jax.numpy as jnp
from jax import lax
from jax.experimental import pallas as pl
from jax.experimental.pallas import tpu as pltpu
from jax.sharding import PartitionSpec as P

WIN = 512
fast_rate = 0.01
epsilon = 1e-06
CORES = 2


def mm(a, b, ca, cb):
    return lax.dot_general(
        a, b, (((ca,), (cb,)), ((), ())), preferred_element_type=jnp.float32
    )


def grad_kernel(renewed, info_ref, coef_ref, keys_ref, targets_ref, scaled_ref, w_ref, *rest):
    if renewed:
        g_ref, out_ref = rest
    else:
        (out_ref,) = rest
    head = pl.program_id(0)

    @pl.when(info_ref[0] == 0)
    def _():
        out_ref[...] = jnp.zeros_like(out_ref)

    @pl.when(info_ref[0] != 0)
    def _():
        def weight(i):
            w = w_ref[0, i]
            if renewed:
                w = w - coef_ref[0] * g_ref[0, i].astype(jnp.float32)
            return w.astype(jnp.bfloat16)

        x = keys_ref[...]
        column = lax.broadcasted_iota(jnp.int32, scaled_ref.shape, 1)
        scaled = jnp.sum(
            jnp.where(column == head, scaled_ref[...], 0.0), axis=1, keepdims=True
        )
        first = mm(x, weight(0), 1, 0)
        third = mm(x, weight(1), 1, 0)
        d_out = (-scaled * targets_ref[...].astype(jnp.float32)).astype(jnp.bfloat16)
        d_act = mm(d_out, weight(2), 1, 0)
        sigma = jax.nn.sigmoid(first)
        swish = first * sigma
        act = (swish * third).astype(jnp.bfloat16)
        d_first = (d_act * third * sigma * (1.0 + first * (1.0 - sigma))).astype(jnp.bfloat16)
        d_third = (d_act * swish).astype(jnp.bfloat16)
        out_ref[0, 0] = mm(x, d_first, 0, 0).astype(jnp.bfloat16)
        out_ref[0, 1] = mm(x, d_third, 0, 0).astype(jnp.bfloat16)
        out_ref[0, 2] = mm(d_out, act, 0, 0).astype(jnp.bfloat16)


def gradients(info, coef, keys, targets, scaled, weights, g):
    local = keys.shape[0]
    heads, _, hd, hid = weights.shape
    wspec = pl.BlockSpec((1, 3, hd, hid), lambda h: (h, 0, 0, 0))
    smem = pl.BlockSpec(memory_space=pltpu.SMEM)
    col = pl.BlockSpec((local, hd), lambda h: (0, h))
    args = [info, coef, keys, targets, scaled, weights]
    specs = [smem, smem, col, col, pl.BlockSpec(scaled.shape, lambda h: (0, 0)), wspec]
    if g is not None:
        args.append(g)
        specs.append(wspec)
    return pl.pallas_call(
        functools.partial(grad_kernel, g is not None),
        grid=(heads,),
        in_specs=specs,
        out_specs=wspec,
        out_shape=jax.ShapeDtypeStruct(weights.shape, jnp.bfloat16),
        compiler_params=pltpu.CompilerParams(vmem_limit_bytes=56 << 20),
        cost_estimate=pl.CostEstimate(
            flops=12 * heads * local * hd * hid, bytes_accessed=30 << 20, transcendentals=0
        ),
        name="grad",
    )(*args)


def attention_kernel(head, chained, info_ref, win_ref, q_ref, k_ref, kh_ref, v_ref, vh_ref, *rest):
    out_ref = rest[-1]
    local, hd = q_ref.shape
    block = 256
    width = win_ref[head]
    anchor = info_ref[2]
    k_all = jnp.concatenate([kh_ref[...], k_ref[...]], axis=0)
    v_all = jnp.concatenate([vh_ref[...], v_ref[...]], axis=0)
    span = WIN + block
    for start in range(0, local, block):
        scores = mm(q_ref[start : start + block], k_all[start : start + span], 1, 1) * (
            hd ** (-0.5)
        )
        row = lax.broadcasted_iota(jnp.int32, (block, span), 0)
        colm = lax.broadcasted_iota(jnp.int32, (block, span), 1)
        back = row + WIN - colm
        live = (back >= 0) & (back < width) & (colm >= WIN - start - anchor)
        scores = jnp.where(live, scores, -1e30)
        peak = jnp.max(scores, axis=1, keepdims=True)
        expo = jnp.exp(scores - peak)
        probs = (expo * (1.0 / jnp.sum(expo, axis=1, keepdims=True))).astype(jnp.bfloat16)
        out_ref[start : start + block] = mm(probs, v_all[start : start + span], 1, 0)


def attention(head, prev, info, window, q, k, kh, v, vh, heads):
    local = q.shape[0]
    hd = q.shape[1] // heads
    smem = pl.BlockSpec(memory_space=pltpu.SMEM)
    col = pl.BlockSpec((local, hd), lambda i: (0, head))
    halo = pl.BlockSpec((WIN, hd), lambda i: (0, head))
    args = [info, window, q, k, kh, v, vh]
    specs = [smem, smem, col, col, halo, col, halo]
    aliases = {}
    if prev is not None:
        args.append(prev)
        specs.append(pl.BlockSpec(memory_space=pl.ANY))
        aliases = {len(args) - 1: 0}
    return pl.pallas_call(
        functools.partial(attention_kernel, head, prev is not None),
        grid=(1,),
        in_specs=specs,
        out_specs=col,
        out_shape=jax.ShapeDtypeStruct(q.shape, jnp.float32),
        input_output_aliases=aliases,
        compiler_params=pltpu.CompilerParams(vmem_limit_bytes=40 << 20),
        cost_estimate=pl.CostEstimate(
            flops=6 * 4 * local * 768 * hd, bytes_accessed=8 << 20, transcendentals=0
        ),
        name="attend",
    )(*args)


def mix_kernel(info_ref, coef_ref, q_ref, attn_ref, w_ref, g_ref, out_ref, y_ref):
    position = info_ref[2] + lax.broadcasted_iota(jnp.int32, (q_ref.shape[0], 1), 0)
    for c in range(2):

        @pl.when(info_ref[c] != 0)
        def _():
            def weight(i):
                w = w_ref[0, i]
                if c:
                    w = w - coef_ref[0] * g_ref[0, i].astype(jnp.float32)
                return w.astype(jnp.bfloat16)

            q = q_ref[...]
            first = mm(q, weight(0), 1, 0)
            third = mm(q, weight(1), 1, 0)
            act = (first * jax.nn.sigmoid(first) * third).astype(jnp.bfloat16)
            y = mm(act, weight(2), 1, 1)
            mine = (position < info_ref[3]) == (c == 0)
            y_ref[...] = jnp.where(mine, y, y_ref[...])

    y = y_ref[...]
    mean = jnp.mean(y * y, axis=1, keepdims=True)
    out_ref[...] = (attn_ref[...] + y / jnp.sqrt(mean + epsilon)).astype(jnp.bfloat16)


def mix(info, coef, q, attn, weights, g):
    local = q.shape[0]
    heads, _, hd, hid = weights.shape
    wspec = pl.BlockSpec((1, 3, hd, hid), lambda h: (h, 0, 0, 0))
    smem = pl.BlockSpec(memory_space=pltpu.SMEM)
    col = pl.BlockSpec((local, hd), lambda h: (0, h))
    return pl.pallas_call(
        mix_kernel,
        grid=(heads,),
        in_specs=[smem, smem, col, col, wspec, wspec],
        out_specs=col,
        out_shape=jax.ShapeDtypeStruct(q.shape, jnp.bfloat16),
        scratch_shapes=[pltpu.VMEM((local, hd), jnp.float32)],
        compiler_params=pltpu.CompilerParams(vmem_limit_bytes=56 << 20),
        cost_estimate=pl.CostEstimate(
            flops=8 * heads * local * hd * hid, bytes_accessed=30 << 20, transcendentals=0
        ),
        name="mix",
    )(info, coef, q, attn, weights, g)


def add_rows(dst, parts):
    rows = dst.shape[0]
    tile = 64 if rows % 64 == 0 else 16

    @pl.loop(0, rows // tile)
    def _(i):
        at = pl.ds(pl.multiple_of(i * tile, tile), tile)
        total = parts[0][at].astype(jnp.float32)
        for part in parts[1:]:
            total += part[at].astype(jnp.float32)
        dst[at] = total.astype(dst.dtype)


def reduce_kernel(near_size, far_size, g_ref, out_ref, sq_ref, r1, s1, rn, sn, rf, sf, send, recv):
    me = lax.axis_index("seq")
    strides = (1, CORES, CORES * near_size)
    sizes = (CORES, near_size, far_size)
    places = tuple((me // st) % sz for st, sz in zip(strides, sizes))
    core, near, far = places

    def peer(axis, d):
        p = places[axis]
        return me + ((p + d + sizes[axis]) % sizes[axis] - p) * strides[axis]

    barrier = pltpu.get_barrier_semaphore()
    total = 0
    for axis in range(3):
        for d in range(1, sizes[axis]):
            pl.semaphore_signal(
                barrier,
                inc=1,
                device_id={"seq": peer(axis, d)},
                device_id_type=pl.DeviceIdType.MESH,
            )
            total += 1
    pl.semaphore_wait(barrier, total)

    used = [0]

    def copy(src, dst, axis, d):
        k = used[0]
        used[0] += 1
        c = pltpu.make_async_remote_copy(
            src_ref=src,
            dst_ref=dst,
            send_sem=send.at[k],
            recv_sem=recv.at[k],
            device_id={"seq": peer(axis, d)},
            device_id_type=pl.DeviceIdType.MESH,
        )
        c.start()
        return c

    half = g_ref.shape[0] // CORES
    width = g_ref.shape[1] // 2

    def rows(start, size):
        return pl.ds(pl.multiple_of(start, 16), size)

    fine = width // 2
    ways = ((0, 1), (1, -1))

    def scatter(axis, src, got, dst):
        size = sizes[axis]
        step = src.shape[0] // size
        place = places[axis]

        def piece(index):
            return src.at[rows(((index + 2 * size) % size) * step, step)]

        if axis == 1:
            cs = [copy(piece(place + d), got.at[d - 1, pl.ds(0, step)], axis, d) for d in range(1, size)]
            yield
            for c in cs:
                c.wait()
            add_rows(dst, [piece(place)] + [got.at[d - 1, pl.ds(0, step)] for d in range(1, size)])
            return
        for s in range(size - 1):
            cs = []
            for i, sign in ways:
                cols = pl.ds(i * fine, fine)
                if s == 0:
                    held = piece(place - sign).at[:, cols]
                else:
                    held = got.at[s - 1, pl.ds(0, step), cols]
                cs.append(copy(held, got.at[s, pl.ds(0, step), cols], axis, sign))
            yield
            for (i, sign), c in zip(ways, cs):
                cols = pl.ds(i * fine, fine)
                c.wait()
                held = got.at[s, pl.ds(0, step), cols]
                own = piece(place - sign * (2 + s)).at[:, cols]
                add_rows(dst.at[:, cols] if s == size - 2 else held, [held, own])

    def gather(axis, base, step, start):
        size = sizes[axis]
        place = places[axis]

        def block(index, first, count):
            at = base + ((index + size) % size) * step
            return out_ref.at[rows(at, step), pl.ds(start + first, count)]

        if axis == 1:
            mine = block(place, 0, width)
            cs = [copy(mine, mine, axis, d) for d in range(1, size)]
            yield
            for c in cs:
                c.wait()
            return
        for s in range(size - 1):
            cs = []
            for i, sign in ways:
                held = block(place - sign * s, i * fine, fine)
                cs.append(copy(held, held, axis, sign))
            yield
            for c in cs:
                c.wait()

    def chain(w):
        cols = pl.ds(w * width, width)
        other = (core + 1) % CORES
        c = copy(g_ref.at[rows(other * half, half), cols], r1.at[w], 0, 1)
        yield
        c.wait()
        add_rows(s1.at[w], [g_ref.at[rows(core * half, half), cols], r1.at[w]])
        a1, a2 = ((1, 2), (2, 1))[w]
        got = {1: rn, 2: rf}
        block = half // sizes[a1]
        small = block // sizes[a2]
        mid = (sn if w == 0 else sf).at[pl.ds(0, block)]
        yield from scatter(a1, s1.at[w], got[a1].at[w], mid)
        base = core * half + places[a1] * block
        own = out_ref.at[rows(base + places[a2] * small, small), cols]
        yield from scatter(a2, mid, got[a2].at[w], own)
        yield from gather(a2, base, small, w * width)
        yield from gather(a1, core * half, block, w * width)
        mine = out_ref.at[rows(core * half, half), cols]
        c = copy(mine, mine, 0, 1)
        yield
        c.wait()

    more = far_size - 2
    halves = (chain(0), chain(1))
    order = [0, 1, 0, 1] + [1] * more + [0, 1] + [0] * more + [1, 0] + [0] * more
    order += [1, 0] + [1] * more + [1, 0, 0, 1]
    for w in order:
        next(halves[w], None)
    assert all(next(c, order) is order for c in halves)
    tile = 64

    def square(i, total):
        at = pl.ds(pl.multiple_of(i * tile, tile), tile)
        part = jnp.square(out_ref[at].astype(jnp.float32))
        return total + jnp.sum(part.reshape(tile // 8, 8, -1), axis=0)

    sq_ref[...] = lax.fori_loop(
        0, out_ref.shape[0] // tile, square, jnp.zeros(sq_ref.shape, jnp.float32)
    )


def summed(ident, grads, total_count):
    count = lax.axis_size("seq")
    chips = count // CORES
    near = 1
    while near * near * 4 <= chips:
        near *= 2
    far = chips // near
    flat = grads.reshape(-1, grads.shape[-1])
    half = flat.shape[0] // CORES
    width = flat.shape[1] // 2
    copies = 4 + 4 * (near - 1) + 8 * (far - 1)
    vm = lambda *shape: pltpu.VMEM(shape, jnp.bfloat16)
    vmem = pl.BlockSpec(memory_space=pltpu.VMEM)
    out, squares = pl.pallas_call(
        functools.partial(reduce_kernel, near, far),
        in_specs=[vmem],
        out_specs=(vmem, vmem),
        out_shape=(
            jax.ShapeDtypeStruct(flat.shape, flat.dtype),
            jax.ShapeDtypeStruct((8, flat.shape[1]), jnp.float32),
        ),
        scratch_shapes=[
            vm(2, half, width),
            vm(2, half, width),
            vm(2, max(near - 1, 1), half // near, width),
            vm(half // near, width),
            vm(2, max(far - 1, 1), half // far, width),
            vm(half // far, width),
            pltpu.SemaphoreType.DMA((copies,)),
            pltpu.SemaphoreType.DMA((copies,)),
        ],
        compiler_params=pltpu.CompilerParams(
            collective_id=ident, has_side_effects=True, vmem_limit_bytes=58 << 20
        ),
        cost_estimate=pl.CostEstimate(
            flops=10**11, bytes_accessed=4 * flat.size, transcendentals=0
        ),
        name="reduce",
    )(flat)
    square = lax.psum(jnp.sum(squares), "head")
    factor = fast_rate / jnp.sqrt(square / total_count + epsilon)
    return out.reshape(grads.shape), factor


def per_device(queries, keys, values, targets, token_rate, window, split, fast_init):
    local = queries.shape[0]
    heads = fast_init.shape[0]
    count = lax.axis_size("seq")
    total_count = float(fast_init.size * lax.axis_size("head"))
    anchor = (lax.axis_index("seq") * local).astype(jnp.int32)
    edge = split[0]
    early = (anchor < edge).astype(jnp.int32)
    late = (anchor + local > edge).astype(jnp.int32)
    info = jnp.stack([early, late, anchor, edge])
    info_late = jnp.stack([late, late, anchor, edge])
    positions = anchor + jnp.arange(local, dtype=jnp.int32)[:, None]
    first_block = (positions < edge).astype(jnp.float32)

    forward = [(i, i + 1) for i in range(count - 1)]
    key_halo = lax.ppermute(keys[local - WIN :], "seq", forward)
    value_halo = lax.ppermute(values[local - WIN :], "seq", forward)

    zero = jnp.zeros((1,), jnp.float32)
    g0 = gradients(info, zero, keys, targets, token_rate * first_block, fast_init, None)
    g0, c0 = summed(0, g0, total_count)
    c0, key_halo, value_halo = lax.optimization_barrier((c0, key_halo, value_halo))
    attn = None
    for head in range(heads):
        attn = attention(
            head, attn, info, window, queries, keys, key_halo, values, value_halo, heads
        )
    coef = c0.reshape(1)
    g1 = gradients(
        info_late, coef, keys, targets, token_rate * (1.0 - first_block), fast_init, g0
    )
    g1, c1 = summed(1, g1, total_count)
    mixed = mix(info, coef, queries, attn, fast_init, g0)
    weights = fast_init - c0 * g0.astype(jnp.float32) - c1 * g1.astype(jnp.float32)
    return mixed, weights


def solution(mesh):
    return jax.shard_map(
        per_device,
        mesh=mesh,
        in_specs=(
            P("seq", "head"),
            P("seq", "head"),
            P("seq", "head"),
            P("seq", "head"),
            P("seq", "head"),
            P("head"),
            P(),
            P("head", None, None, None),
        ),
        out_specs=(P("seq", "head"), P("head", None, None, None)),
        check_vma=False,
    )
```
